32 devices in a mesh: group: 2 (over core), dp: 4 (over z), section: 2 (over x), tensor: 2 (over y).
Axes of the slice: x: 2, y: 2, z: 4, core: 2. Of those that a mesh axis runs over, the one named last changes fastest.
Arguments:
- merged: bfloat16 [768, 5120], P('dp'), may hold values from -6 to 6
- counts: int32 [8], P('dp'), may hold values from 4 to 384
- owners: int32 [768, 1], P('dp'), may hold values from 0 to 3; in each aligned block of 192 rows (0 to 191, 192 to 383, ...) at most 96 rows name the same one
- w_merge: bfloat16 [5120, 8192], P(None, ('group', 'section', 'tensor')), may hold values from -0.078125 to 0.078125
- norm_gain: float32 [8192], P(('group', 'section', 'tensor')), may hold values from 0.25 to 1.75
- cotangent: bfloat16 [4, 4, 96, 8192], P('dp', None, None, ('group', 'section', 'tensor')), may hold values from -6 to 6
Outputs:
- embedded: bfloat16 [4, 4, 96, 8192], P('dp', None, None, ('group', 'section', 'tensor'))
- grad_merged: float32 [768, 5120], P('dp', ('group', 'section', 'tensor'))
- grad_weight: float32 [5120, 8192], P('dp', ('group', 'section', 'tensor'))
The draws below stay inside these ranges and needn't reach their ends.
Inputs may be any that keep to these rules, and one draw needn't show every extreme that they name: `owners`: in each replica's 192 rows no owner appears more than 96 times.
All inputs are finite; a program needn't handle non-finite values.
Results may differ from the reference program's by a relative error of at most 0.0049.
Values may be sent and summed in bfloat16 or wider, within the bound.
A program may use at most 64 MiB of HBM per device.

```python
import math
import jax
import jax.numpy as jnp
import numpy as np
from jax import lax

D = 8192
DM = 5120
ROWS = 192
SAMP = 2
SLOT = 96
MOST = 96
N_DP = 4


def set_ends(values, key, smallest, top_value):
    place = [jax.random.randint(jax.random.fold_in(key, axis), (), 0, length) for axis, length in enumerate(values.shape)]
    widest = values.shape.index(max(values.shape))
    next_to = place[:widest] + [(place[widest] + 1) % values.shape[widest]] + place[widest + 1:]
    return values.at[tuple(place)].set(smallest).at[tuple(next_to)].set(top_value)


def block_scale(rng, dims, shards, least, largest):
    def one(dim, shards_of):
        steps = jax.random.uniform(jax.random.fold_in(jax.random.fold_in(rng, 6), dim), (shards_of,), jnp.float32, least / len(shards), largest / len(shards))
        return jnp.repeat(jnp.exp(steps), dims[dim] // shards_of).reshape((-1,) + (1,) * (len(dims) - dim - 1))

    gain = one(*shards[0])
    for cut in shards[1:]:
        gain = gain * one(*cut)
    return gain


def assign_block(stream_key, own, number, rows, count, top, most, lean):
    order = jax.random.permutation(stream_key, count)
    heavy_load, usual = shares(count, rows * top, most, lean, True), shares(count, rows * top, most, lean, False)
    places = jnp.arange(count)

    def named(tallies, offset_by):
        used = int((tallies > 0).sum())
        fixed = max(1, used // 4)
        passed = fixed + (places - fixed + offset_by * (used - fixed)) % max(1, count - fixed)
        return jnp.zeros((count,), jnp.int32).at[order[jnp.where(places < fixed, places, passed)]].set(jnp.asarray(tallies, jnp.int32))

    tallies = jnp.where(number % 4 == 0, named(heavy_load, number // 4), named(usual, number - number // 4 - 1))
    mixed = jax.random.permutation(jax.random.fold_in(own, 3), count)
    donor, sink = mixed[0:count // 2 * 2:2], mixed[1:count // 2 * 2:2]
    room = jnp.minimum(tallies[donor] - 1, most - tallies[sink]) // 2
    room = jnp.where((donor == order[0]) | (sink == order[0]) | (tallies[sink] == 0), 0, jnp.maximum(room, 0))
    passed = jax.random.randint(jax.random.fold_in(own, 4), (count // 2,), 0, 1 << 20) % (room + 1)
    tallies = tallies.at[donor].add(-passed).at[sink].add(passed)
    items = jnp.searchsorted(jnp.cumsum(tallies), jnp.arange(rows * top), side="right").astype(jnp.int32)
    table = items.reshape(top, rows).T
    table = table[jax.random.permutation(jax.random.fold_in(own, 1), rows)]
    offset_by = jax.random.randint(jax.random.fold_in(own, 2), (rows, 1), 0, top)
    return jnp.take_along_axis(table, (jnp.arange(top)[None, :] + offset_by) % top, axis=1)


def shares(amount, total, limit, slope, full):
    portions = [(1 << 20) // math.isqrt(rank ** slope) + 1 for rank in range(1, amount + 1)]
    largest = limit if full else min(limit, max(-(-total // amount), total * portions[0] // sum(portions)))
    least = 1 if total - largest >= amount - 1 else 0
    given, spare = [largest] + [least] * (amount - 1), total - largest - least * (amount - 1)
    while spare > 0:
        candidates = [i for i in range(1, amount) if given[i] < largest] or [i for i in range(1, amount) if given[i] < limit]
        pool, left = sum([portions[i] for i in candidates]), spare
        for i in candidates:
            extra = min(limit - given[i], max(1, left * portions[i] // pool), spare)
            given[i] = given[i] + extra
            spare = spare - extra
    return np.array(given)


def centred(key, dims, spread, most, split=(), kind=jnp.bfloat16):
    drawn = jax.random.normal(key, dims, jnp.float32) * spread
    if len(split) > 0:
        drawn = block_scale(key, dims, split, -0.22, 0.18) * drawn
    return jnp.clip(drawn, min=-most, max=most).astype(kind)


def setup_inputs(seed: int = 0) -> dict:
    key_list = jax.random.split(jax.random.key(seed), 7)
    merged = centred(key_list[0], (N_DP * ROWS, DM), 1.0, 6.0, ((0, 4),))
    counts = set_ends(jax.random.randint(key_list[1], (N_DP * SAMP,), 4, 4 * SLOT + 1), jax.random.fold_in(key_list[1], 1), 4, 4 * SLOT).astype(jnp.int32)
    owners_keys = jax.random.split(jax.random.fold_in(key_list[2], 1), (N_DP * ROWS) // ROWS)
    owners_turns = jax.random.permutation(jax.random.fold_in(key_list[2], 3), (N_DP * ROWS) // ROWS)
    owners = jax.vmap(lambda own, number: assign_block(jax.random.fold_in(key_list[2], 2), own, number, ROWS, N_DP, 1, MOST, 2))(owners_keys, owners_turns).reshape((N_DP * ROWS, 1))
    w_merge = centred(key_list[3], (DM, D), DM ** -0.5, 0.078125, ((1, 8),))
    norm_gain = jnp.clip(1.0 + 0.15 * jax.random.normal(key_list[4], (D,), jnp.float32), 0.25, 1.75)
    cotangent = centred(key_list[5], (N_DP, N_DP, MOST, D), 1.0, 6.0, ((0, 4), (3, 8)))
    return {"merged": merged, "counts": counts, "owners": owners, "w_merge": w_merge, "norm_gain": norm_gain, "cotangent": cotangent}


def reference(merged, counts, owners, w_merge, norm_gain, cotangent):
    total = merged.shape[0]
    projected = jnp.dot(merged, w_merge, preferred_element_type=jnp.float32).astype(jnp.bfloat16)
    row_index = jnp.arange(total, dtype=jnp.int32)
    within = row_index % ROWS
    image = row_index // ROWS * SAMP + within // SLOT
    valid = (4 * (within % SLOT) < counts[image]).astype(jnp.float32)
    masked = (projected.astype(jnp.float32) * valid[:, None]).astype(jnp.bfloat16)
    owner = owners[:, 0].astype(jnp.int32)
    hits = (owner[:, None] == jnp.arange(N_DP, dtype=jnp.int32)[None, :]).astype(jnp.int32)
    blocked = hits.reshape(N_DP, ROWS, N_DP)
    before = jnp.cumsum(blocked, axis=1) - blocked
    slot_index = lax.optimization_barrier(jnp.sum(before * blocked, axis=2)).reshape(total).astype(jnp.int32)
    block = (row_index // ROWS).astype(jnp.int32)
    values = masked.astype(jnp.float32)
    scale = jax.lax.rsqrt(lax.optimization_barrier(jnp.mean(values * values, axis=1)) + 1e-05)
    normed = (values * scale[:, None] * norm_gain[None, :]).astype(jnp.bfloat16)
    embedded = jnp.zeros((N_DP, N_DP, MOST, D), jnp.bfloat16).at[owner, block, slot_index].set(normed)
    grad_in = cotangent[owner, block, slot_index].astype(jnp.float32) * norm_gain[None, :]
    inner = lax.optimization_barrier(jnp.mean(grad_in * values, axis=1))
    back = (scale[:, None] * grad_in - values * (scale ** 3 * inner)[:, None]).astype(jnp.bfloat16)
    back = (back.astype(jnp.float32) * valid[:, None]).astype(jnp.bfloat16)
    grad_merged = jnp.dot(back, w_merge.T, preferred_element_type=jnp.float32)
    grad_weight = jnp.dot(merged.T, back, preferred_element_type=jnp.float32)
    return (embedded, grad_merged, grad_weight)
```

```python
import functools

import jax
import jax.numpy as jnp
from jax import lax
from jax.experimental import pallas as pl
from jax.experimental.pallas import tpu as pltpu
from jax.sharding import PartitionSpec as P

D = 8192
MESH = pl.DeviceIdType.MESH
F32 = jnp.float32
BF16 = jnp.bfloat16
WCHUNKS = 5
BCHUNKS = 4


def on_device(merged, counts, owners, w_merge, norm_gain, cotangent):
    rows = merged.shape[0]
    columns = w_merge.shape[1]
    replicas = lax.axis_size("dp")
    slots = cotangent.shape[2]
    images = counts.shape[0]
    per_image = rows // images
    projected = jnp.dot(merged, w_merge, preferred_element_type=jnp.float32).astype(jnp.bfloat16)
    row_index = jnp.arange(rows, dtype=jnp.int32)
    image_of = row_index // per_image
    picked = image_of[:, None] == jnp.arange(images, dtype=jnp.int32)[None, :]
    count_of = jnp.sum(jnp.where(picked, counts[None, :], 0), axis=1)
    valid = (4 * (row_index % per_image) < count_of).astype(jnp.float32)
    masked = (projected.astype(jnp.float32) * valid[:, None]).astype(jnp.bfloat16)
    owner = owners[:, 0]
    hits = (owner[:, None] == jnp.arange(replicas, dtype=jnp.int32)[None, :]).astype(jnp.int32)
    before = jnp.cumsum(hits, axis=0) - hits
    slot_index = jnp.sum(before * hits, axis=1)
    target = owner * slots + slot_index
    placer = (jnp.arange(replicas * slots, dtype=jnp.int32)[:, None] == target[None, :]).astype(
        jnp.bfloat16
    )
    outgoing = jnp.dot(placer, masked, preferred_element_type=jnp.float32).astype(jnp.bfloat16)
    outgoing = outgoing.reshape(replicas, slots, columns)
    received = lax.all_to_all(outgoing, "dp", split_axis=0, concat_axis=0, tiled=True)
    values = received.astype(jnp.float32)
    square_sums = lax.psum(jnp.sum(values * values, axis=2), ("group", "section", "tensor"))
    scale = lax.rsqrt(square_sums / D + 1e-05)
    normed = (values * scale[:, :, None] * norm_gain[None, None, :]).astype(jnp.bfloat16)
    embedded = normed[None]
    grad_in = cotangent[0].astype(jnp.float32) * norm_gain[None, None, :]
    inner_sums = lax.psum(jnp.sum(grad_in * values, axis=2), ("group", "section", "tensor"))
    inner = inner_sums / D
    slot_grad = (scale[:, :, None] * grad_in - values * (scale**3 * inner)[:, :, None]).astype(
        jnp.bfloat16
    )
    returned = lax.all_to_all(slot_grad, "dp", split_axis=0, concat_axis=0, tiled=True)
    returned = returned.reshape(replicas * slots, columns)
    gathered = lax.dot_general(
        placer, returned, (((0,), (0,)), ((), ())), preferred_element_type=jnp.float32
    )
    back = (gathered * valid[:, None]).astype(jnp.bfloat16)
    input_terms = lax.dot_general(
        back, w_merge, (((1,), (1,)), ((), ())), preferred_element_type=jnp.float32
    )
    grad_merged = lax.psum_scatter(
        input_terms, ("group", "section", "tensor"), scatter_dimension=1, tiled=True
    )
    column_block = lax.all_to_all(merged, "dp", split_axis=1, concat_axis=0, tiled=True)
    grad_weight = lax.dot_general(
        column_block,
        lax.all_gather(back, "dp", axis=0, tiled=True),
        (((0,), (0,)), ((), ())),
        preferred_element_type=jnp.float32,
    )
    return (embedded, grad_merged, grad_weight)


def remote(src, dst, send_sem, recv_sem, device):
    return pltpu.make_async_remote_copy(
        src_ref=src,
        dst_ref=dst,
        send_sem=send_sem,
        recv_sem=recv_sem,
        device_id=device,
        device_id_type=MESH,
    )


def main_kernel(
    sizes,
    own_col,
    own_row,
    counts,
    merged,
    w_hbm,
    gain_ref,
    cot,
    emb,
    gm,
    mblk,
    back_all,
    w,
    cot_in,
    outgoing,
    masked,
    stat_out,
    stat_in,
    pair_out,
    pair_in,
    plane_out,
    plane_in,
    w_sem,
    zm_s,
    zm_r,
    zc_s,
    zc_r,
    ze_s,
    ze_r,
    st_s,
    st_r,
    pm_s,
    pm_r,
    gm_s,
    gm_r,
    bk_s,
    bk_r,
    po_s,
    po_r,
    pl_s,
    pl_r,
):
    n, groups, sections, tensors = sizes
    plane = sections * tensors
    shards = groups * plane
    rows, deep = merged.shape
    cols = w.shape[1]
    slots = cot.shape[1]
    dblock = deep // n
    half = dblock // groups
    part = rows // plane
    gcols = deep // shards
    images = counts.shape[0]
    per_image = rows // images
    me = lax.axis_index("dp")
    g = lax.axis_index("group")
    st = lax.axis_index("section") * tensors + lax.axis_index("tensor")
    f = g * plane + st

    def dp_of(r):
        return lax.rem(me + r, n)

    def at_plane(gg, ss):
        return {"group": gg, "section": ss // tensors, "tensor": lax.rem(ss, tensors)}

    barrier = pltpu.get_barrier_semaphore()
    for r in range(1, n):
        pl.semaphore_signal(barrier, inc=1, device_id={"dp": dp_of(r)}, device_id_type=MESH)
    for q in range(1, shards):
        other = lax.rem(f + q, shards)
        pl.semaphore_signal(
            barrier,
            inc=1,
            device_id=at_plane(other // plane, lax.rem(other, plane)),
            device_id_type=MESH,
        )
    wrows = deep // WCHUNKS
    wcopies = []
    for c in range(WCHUNKS):
        copy = pltpu.make_async_copy(
            w_hbm.at[pl.ds(c * wrows, wrows), :], w.at[pl.ds(c * wrows, wrows), :], w_sem.at[c]
        )
        copy.start()
        wcopies.append(copy)
    pl.semaphore_wait(barrier, n - 1 + shards - 1)

    my_rows = pl.ds(pl.multiple_of(st * part, part), part)
    my_cols = pl.ds(pl.multiple_of(g * half, half), half)
    zm = []
    zc = []
    for r in range(1, n):
        to = dp_of(r)
        copy = remote(
            merged.at[my_rows, pl.ds(pl.multiple_of(to * dblock + g * half, half), half)],
            mblk.at[me, my_rows, my_cols],
            zm_s.at[r - 1],
            zm_r.at[r - 1],
            {"dp": to},
        )
        copy.start()
        zm.append(copy)
    for r in range(1, n):
        to = dp_of(r)
        copy = remote(cot.at[to], cot_in.at[n - r], zc_s.at[r - 1], zc_r.at[n - r - 1], {"dp": to})
        copy.start()
        zc.append(copy)

    acc = jnp.zeros((rows, cols), F32)
    for c in range(WCHUNKS):
        wcopies[c].wait()
        acc = acc + jnp.dot(
            merged[:, c * wrows : (c + 1) * wrows],
            w[c * wrows : (c + 1) * wrows, :],
            preferred_element_type=F32,
        )

    row_of = lax.broadcasted_iota(jnp.int32, (rows, 1), 0)
    valid = jnp.zeros((rows, 1), F32)
    for im in range(images):
        inside = (row_of >= im * per_image) & (row_of < (im + 1) * per_image)
        seen = inside & (4 * (row_of - im * per_image) < counts[im])
        valid = jnp.where(seen, 1.0, valid)
    masked[...] = acc.astype(BF16).astype(F32) * valid
    values = masked[...]

    wide = stat_out.shape[2]
    eye = lax.broadcasted_iota(jnp.int32, (rows, wide), 0) == lax.broadcasted_iota(
        jnp.int32, (rows, wide), 1
    )

    def send_stat(which, column):
        line = jnp.sum(jnp.where(eye, column, 0.0), axis=0, keepdims=True)
        line = jnp.broadcast_to(line, (8, wide))
        stat_out[which] = line
        stat_in[which, f] = line
        copies = []
        for q in range(1, shards):
            other = lax.rem(f + q, shards)
            copy = remote(
                stat_out.at[which],
                stat_in.at[which, f],
                st_s.at[which, q - 1],
                st_r.at[which, q - 1],
                at_plane(other // plane, lax.rem(other, plane)),
            )
            copy.start()
            copies.append(copy)
        return copies

    def take_stat(which, copies):
        for copy in copies:
            copy.wait()
        line = stat_in[which, 0]
        for other in range(1, shards):
            line = line + stat_in[which, other]
        return jnp.sum(jnp.where(eye, line[0:1], 0.0), axis=1, keepdims=True)

    squares = send_stat(0, jnp.sum(values * values, axis=1, keepdims=True))

    oc = own_col[...]
    orow = own_row[...]
    hits_c = (oc == lax.broadcasted_iota(jnp.int32, (rows, n), 1)).astype(F32)
    hits_r = (orow == lax.broadcasted_iota(jnp.int32, (n, rows), 0)).astype(F32)
    i0 = lax.broadcasted_iota(jnp.int32, (rows, rows), 0)
    i1 = lax.broadcasted_iota(jnp.int32, (rows, rows), 1)
    lower = (i1 < i0).astype(F32).astype(BF16)
    upper = (i0 < i1).astype(F32).astype(BF16)
    before_c = jnp.dot(lower, hits_c.astype(BF16), preferred_element_type=F32)
    before_r = jnp.dot(hits_r.astype(BF16), upper, preferred_element_type=F32)
    slot_c = jnp.sum(before_c * hits_c, axis=1, keepdims=True).astype(jnp.int32)
    slot_r = jnp.sum(before_r * hits_r, axis=0, keepdims=True).astype(jnp.int32)
    rel_c = jnp.where(oc < me, oc - me + n, oc - me)
    rel_r = jnp.where(orow < me, orow - me + n, orow - me)
    tgt_c = rel_c * slots + slot_c
    tgt_r = rel_r * slots + slot_r
    gain = gain_ref[...]

    mblk[me] = merged[:, pl.ds(pl.multiple_of(me * dblock, dblock), dblock)]

    scale = lax.rsqrt(take_stat(0, squares) / D + 1e-05)
    normed = (values * scale * gain).astype(BF16)
    ze = []
    for r in range(n):
        place = (
            lax.broadcasted_iota(jnp.int32, (slots, rows), 0) + r * slots == tgt_r
        ).astype(F32).astype(BF16)
        block = jnp.dot(place, normed, preferred_element_type=F32).astype(BF16)
        if r == 0:
            emb[me] = block
        else:
            outgoing[r - 1] = block
            copy = remote(
                outgoing.at[r - 1], emb.at[me], ze_s.at[r - 1], ze_r.at[r - 1], {"dp": dp_of(r)}
            )
            copy.start()
            ze.append(copy)

    pm = []
    for r in range(1, n):
        zm[r - 1].wait()
        source = dp_of(n - r)
        for q in range(1, plane):
            piece = mblk.at[source, my_rows, my_cols]
            copy = remote(
                piece,
                piece,
                pm_s.at[r - 1, q - 1],
                pm_r.at[r - 1, q - 1],
                at_plane(g, lax.rem(st + q, plane)),
            )
            copy.start()
            pm.append(copy)

    for copy in zc:
        copy.wait()
    grads = jnp.zeros((rows, cols), F32)
    for r in range(n):
        place = (
            lax.broadcasted_iota(jnp.int32, (rows, slots), 1) + r * slots == tgt_c
        ).astype(F32).astype(BF16)
        block = cot[me] if r == 0 else cot_in[r]
        grads = grads + jnp.dot(place, block, preferred_element_type=F32)
    grads = grads * gain
    values = masked[...]
    inners = send_stat(1, jnp.sum(grads * values, axis=1, keepdims=True))
    inner = take_stat(1, inners) / D
    back = (scale * grads - values * (scale * scale * scale * inner)).astype(BF16)
    back = (back.astype(F32) * valid).astype(BF16)
    back_all[me] = back

    brows = rows // BCHUNKS

    def hop(j, c, side):
        piece = back_all.at[j, pl.ds(c * brows, brows), :]
        return remote(
            piece,
            piece,
            bk_s.at[side, j, c],
            bk_r.at[j, c],
            {"dp": jnp.clip(me + (1 if side == 0 else -1), 0, n - 1)},
        )

    for c in range(BCHUNKS):

        @pl.when(me < n - 1)
        def _():
            hop(me, c, 0).start()

        @pl.when(me > 0)
        def _():
            hop(me, c, 1).start()

    gm_copies = []
    for r in range(1, n):
        for q in range(1, plane):
            pm[(r - 1) * (plane - 1) + q - 1].wait()
        piece = mblk.at[dp_of(n - r), :, my_cols]
        copy = remote(piece, piece, gm_s.at[r - 1], gm_r.at[r - 1], {"group": 1 - g})
        copy.start()
        gm_copies.append(copy)

    def partial(gg, ss):
        start = pl.multiple_of((gg * plane + ss) * gcols, gcols)
        return lax.dot_general(
            back_all[me],
            w[pl.ds(start, gcols), :],
            (((1,), (1,)), ((), ())),
            preferred_element_type=F32,
        )

    po = []
    for q in range(plane):
        slot = (q + 1) % plane
        pair_out[slot] = partial(1 - g, lax.rem(st + slot, plane)).astype(BF16)
        copy = remote(
            pair_out.at[slot], pair_in.at[slot], po_s.at[slot], po_r.at[slot], {"group": 1 - g}
        )
        copy.start()
        po.append(copy)
    ps = []
    for q in range(plane):
        slot = (q + 1) % plane
        mine = partial(g, lax.rem(st + slot, plane))
        po[q].wait()
        mine = mine + pair_in[slot].astype(F32)
        if slot == 0:
            gm[...] = mine
        else:
            plane_out[slot - 1] = mine.astype(BF16)
            copy = remote(
                plane_out.at[slot - 1],
                plane_in.at[slot - 1],
                pl_s.at[slot - 1],
                pl_r.at[slot - 1],
                at_plane(g, lax.rem(st + slot, plane)),
            )
            copy.start()
            ps.append(copy)

    for t in range(1, n):
        for c in range(BCHUNKS):

            @pl.when(me - t >= 0)
            def _():
                hop(me - t, c, 0).wait_recv()

            @pl.when((me - t >= 0) & (me < n - 1))
            def _():
                hop(me - t, c, 0).start()

            @pl.when(me + t <= n - 1)
            def _():
                hop(me + t, c, 1).wait_recv()

            @pl.when((me + t <= n - 1) & (me > 0))
            def _():
                hop(me + t, c, 1).start()

    for copy in ps:
        copy.wait()
    total = gm[...]
    for q in range(plane - 1):
        total = total + plane_in[q].astype(F32)
    gm[...] = total
    for copy in ze:
        copy.wait()
    for copy in gm_copies:
        copy.wait()
    for t in range(n):
        for c in range(BCHUNKS):

            @pl.when((me - t >= 0) & (me < n - 1))
            def _():
                hop(me - t, c, 0).wait_send()

            @pl.when((me + t <= n - 1) & (me > 0))
            def _():
                hop(me + t, c, 1).wait_send()


def weight_kernel(m_ref, b_ref, o_ref):
    o_ref[...] = lax.dot_general(
        m_ref[...], b_ref[...], (((0,), (0,)), ((), ())), preferred_element_type=F32
    )


def fast(sizes, merged, counts, owners, w_merge, norm_gain, cotangent):
    n, groups, sections, tensors = sizes
    plane = sections * tensors
    shards = groups * plane
    rows, deep = merged.shape
    cols = w_merge.shape[1]
    slots = cotangent.shape[2]
    dblock = deep // n
    gcols = deep // shards
    wide = -(-rows // 128) * 128
    vmem = pl.BlockSpec(memory_space=pltpu.VMEM)
    dma = pltpu.SemaphoreType.DMA
    emb, gm, mblk, back_all = pl.pallas_call(
        functools.partial(main_kernel, sizes),
        name="exchange",
        out_shape=(
            jax.ShapeDtypeStruct((n, slots, cols), BF16),
            jax.ShapeDtypeStruct((rows, gcols), F32),
            jax.ShapeDtypeStruct((n, rows, dblock), BF16),
            jax.ShapeDtypeStruct((n, rows, cols), BF16),
        ),
        in_specs=[
            vmem,
            vmem,
            pl.BlockSpec(memory_space=pltpu.SMEM),
            vmem,
            pl.BlockSpec(memory_space=pl.ANY),
            vmem,
            vmem,
        ],
        out_specs=(vmem, vmem, vmem, vmem),
        scratch_shapes=[
            pltpu.VMEM((deep, cols), BF16),
            pltpu.VMEM((n, slots, cols), BF16),
            pltpu.VMEM((n - 1, slots, cols), BF16),
            pltpu.VMEM((rows, cols), F32),
            pltpu.VMEM((2, 8, wide), F32),
            pltpu.VMEM((2, shards, 8, wide), F32),
            pltpu.VMEM((plane, rows, gcols), BF16),
            pltpu.VMEM((plane, rows, gcols), BF16),
            pltpu.VMEM((plane - 1, rows, gcols), BF16),
            pltpu.VMEM((plane - 1, rows, gcols), BF16),
            dma((WCHUNKS,)),
            dma((n - 1,)),
            dma((n - 1,)),
            dma((n - 1,)),
            dma((n - 1,)),
            dma((n - 1,)),
            dma((n - 1,)),
            dma((2, shards - 1)),
            dma((2, shards - 1)),
            dma((n - 1, plane - 1)),
            dma((n - 1, plane - 1)),
            dma((n - 1,)),
            dma((n - 1,)),
            dma((2, n, BCHUNKS)),
            dma((n, BCHUNKS)),
            dma((plane,)),
            dma((plane,)),
            dma((plane - 1,)),
            dma((plane - 1,)),
        ],
        compiler_params=pltpu.CompilerParams(collective_id=0, has_side_effects=True),
    )(
        owners,
        owners.reshape(1, rows),
        counts,
        merged,
        w_merge,
        norm_gain.reshape(1, cols),
        cotangent[0],
    )
    tile = 256
    grad_weight = pl.pallas_call(
        weight_kernel,
        name="weight",
        grid=(dblock // tile,),
        out_shape=jax.ShapeDtypeStruct((dblock, cols), F32),
        in_specs=[
            pl.BlockSpec((n * rows, tile), lambda i: (0, i)),
            pl.BlockSpec((n * rows, cols), lambda i: (0, 0)),
        ],
        out_specs=pl.BlockSpec((tile, cols), lambda i: (i, 0)),
    )(mblk.reshape(n * rows, dblock), back_all.reshape(n * rows, cols))
    return emb[None], gm, grad_weight


def solution(mesh):
    sizes = tuple(mesh.shape[name] for name in ("dp", "group", "section", "tensor"))

    def choose(merged, counts, owners, w_merge, norm_gain, cotangent):
        n, groups, sections, tensors = sizes
        plane = sections * tensors
        rows, deep = merged.shape
        cols = w_merge.shape[1]
        slots = cotangent.shape[2]
        fits = (
            groups == 2
            and n > 1
            and plane > 1
            and rows % (plane * 16) == 0
            and rows % (BCHUNKS * 16) == 0
            and deep % (n * groups * 128) == 0
            and deep % (n * 256) == 0
            and deep % (groups * plane * 128) == 0
            and deep % (WCHUNKS * 128) == 0
            and cols % 128 == 0
            and slots % 16 == 0
        )
        if fits:
            return fast(sizes, merged, counts, owners, w_merge, norm_gain, cotangent)
        return on_device(merged, counts, owners, w_merge, norm_gain, cotangent)

    placed = (
        P("dp", None),
        P("dp"),
        P("dp", None),
        P(None, ("group", "section", "tensor")),
        P(("group", "section", "tensor")),
        P("dp", None, None, ("group", "section", "tensor")),
    )
    return jax.shard_map(
        choose,
        mesh=mesh,
        in_specs=placed,
        out_specs=(
            P("dp", None, None, ("group", "section", "tensor")),
            P("dp", ("group", "section", "tensor")),
            P("dp", ("group", "section", "tensor")),
        ),
        check_vma=False,
    )
```

```python
import functools

import jax
import jax.numpy as jnp
from jax import lax
from jax.experimental import pallas as pl
from jax.experimental.pallas import tpu as pltpu
from jax.sharding import PartitionSpec as P

D = 8192
MESH = pl.DeviceIdType.MESH
F32 = jnp.float32
BF16 = jnp.bfloat16
WCHUNKS = 5
BCHUNKS = 2


def on_device(merged, counts, owners, w_merge, norm_gain, cotangent):
    rows = merged.shape[0]
    columns = w_merge.shape[1]
    replicas = lax.axis_size("dp")
    slots = cotangent.shape[2]
    images = counts.shape[0]
    per_image = rows // images
    projected = jnp.dot(merged, w_merge, preferred_element_type=jnp.float32).astype(jnp.bfloat16)
    row_index = jnp.arange(rows, dtype=jnp.int32)
    image_of = row_index // per_image
    picked = image_of[:, None] == jnp.arange(images, dtype=jnp.int32)[None, :]
    count_of = jnp.sum(jnp.where(picked, counts[None, :], 0), axis=1)
    valid = (4 * (row_index % per_image) < count_of).astype(jnp.float32)
    masked = (projected.astype(jnp.float32) * valid[:, None]).astype(jnp.bfloat16)
    owner = owners[:, 0]
    hits = (owner[:, None] == jnp.arange(replicas, dtype=jnp.int32)[None, :]).astype(jnp.int32)
    before = jnp.cumsum(hits, axis=0) - hits
    slot_index = jnp.sum(before * hits, axis=1)
    target = owner * slots + slot_index
    placer = (jnp.arange(replicas * slots, dtype=jnp.int32)[:, None] == target[None, :]).astype(
        jnp.bfloat16
    )
    outgoing = jnp.dot(placer, masked, preferred_element_type=jnp.float32).astype(jnp.bfloat16)
    outgoing = outgoing.reshape(replicas, slots, columns)
    received = lax.all_to_all(outgoing, "dp", split_axis=0, concat_axis=0, tiled=True)
    values = received.astype(jnp.float32)
    square_sums = lax.psum(jnp.sum(values * values, axis=2), ("group", "section", "tensor"))
    scale = lax.rsqrt(square_sums / D + 1e-05)
    normed = (values * scale[:, :, None] * norm_gain[None, None, :]).astype(jnp.bfloat16)
    embedded = normed[None]
    grad_in = cotangent[0].astype(jnp.float32) * norm_gain[None, None, :]
    inner_sums = lax.psum(jnp.sum(grad_in * values, axis=2), ("group", "section", "tensor"))
    inner = inner_sums / D
    slot_grad = (scale[:, :, None] * grad_in - values * (scale**3 * inner)[:, :, None]).astype(
        jnp.bfloat16
    )
    returned = lax.all_to_all(slot_grad, "dp", split_axis=0, concat_axis=0, tiled=True)
    returned = returned.reshape(replicas * slots, columns)
    gathered = lax.dot_general(
        placer, returned, (((0,), (0,)), ((), ())), preferred_element_type=jnp.float32
    )
    back = (gathered * valid[:, None]).astype(jnp.bfloat16)
    input_terms = lax.dot_general(
        back, w_merge, (((1,), (1,)), ((), ())), preferred_element_type=jnp.float32
    )
    grad_merged = lax.psum_scatter(
        input_terms, ("group", "section", "tensor"), scatter_dimension=1, tiled=True
    )
    column_block = lax.all_to_all(merged, "dp", split_axis=1, concat_axis=0, tiled=True)
    grad_weight = lax.dot_general(
        column_block,
        lax.all_gather(back, "dp", axis=0, tiled=True),
        (((0,), (0,)), ((), ())),
        preferred_element_type=jnp.float32,
    )
    return (embedded, grad_merged, grad_weight)


def remote(src, dst, send_sem, recv_sem, device):
    return pltpu.make_async_remote_copy(
        src_ref=src,
        dst_ref=dst,
        send_sem=send_sem,
        recv_sem=recv_sem,
        device_id=device,
        device_id_type=MESH,
    )


def main_kernel(
    sizes,
    own_row,
    counts,
    merged,
    w_hbm,
    gain_ref,
    cot_hbm,
    emb,
    gm,
    mblk,
    back_all,
    w,
    cots,
    mix,
    mix_out,
    info,
    masked,
    stat_out,
    stat_in,
    pair_out,
    pair_in,
    plane_out,
    plane_in,
    w_sem,
    cot_sem,
    zm_s,
    zm_r,
    ck_s,
    ck_r,
    in_s,
    in_r,
    st_s,
    st_r,
    pm_s,
    pm_r,
    gm_s,
    gm_r,
    mx_s,
    mx_r,
    po_s,
    po_r,
    pl_s,
    pl_r,
):
    n, groups, sections, tensors = sizes
    plane = sections * tensors
    shards = groups * plane
    rows, deep = merged.shape
    cols = w.shape[1]
    slots = cots.shape[2]
    dblock = deep // n
    half = dblock // groups
    part = rows // plane
    gcols = deep // shards
    images = counts.shape[0]
    per_image = rows // images
    me = lax.axis_index("dp")
    g = lax.axis_index("group")
    st = lax.axis_index("section") * tensors + lax.axis_index("tensor")
    f = g * plane + st

    def dp_of(r):
        return lax.rem(me + r, n)

    def at_plane(gg, ss):
        return {"group": gg, "section": ss // tensors, "tensor": lax.rem(ss, tensors)}

    barrier = pltpu.get_barrier_semaphore()
    for r in range(1, n):
        pl.semaphore_signal(barrier, inc=1, device_id={"dp": dp_of(r)}, device_id_type=MESH)
    for q in range(1, shards):
        other = lax.rem(f + q, shards)
        pl.semaphore_signal(
            barrier,
            inc=1,
            device_id=at_plane(other // plane, lax.rem(other, plane)),
            device_id_type=MESH,
        )
    cot_load = pltpu.make_async_copy(cot_hbm, cots.at[me], cot_sem)
    cot_load.start()
    wrows = deep // WCHUNKS
    wcopies = []
    for c in range(WCHUNKS):
        copy = pltpu.make_async_copy(
            w_hbm.at[pl.ds(c * wrows, wrows), :], w.at[pl.ds(c * wrows, wrows), :], w_sem.at[c]
        )
        copy.start()
        wcopies.append(copy)
    pl.semaphore_wait(barrier, n - 1 + shards - 1)

    my_rows = pl.ds(pl.multiple_of(st * part, part), part)
    my_cols = pl.ds(pl.multiple_of(g * half, half), half)
    def step_to(side):
        return {"dp": jnp.clip(me + (1 if side == 0 else -1), 0, n - 1)}

    def cot_hop(p, b, side):
        piece = cots.at[p, b]
        return remote(piece, piece, ck_s.at[p, b], ck_r.at[p, b], step_to(side))

    cot_load.wait()
    for k in range(n - 1):
        b = n - 1 - k

        @pl.when(me < b)
        def _():
            cot_hop(me, b, 0).start()

        @pl.when(me > k)
        def _():
            cot_hop(me, k, 1).start()

    zm = []
    for r in range(1, n):
        to = dp_of(r)
        copy = remote(
            merged.at[my_rows, pl.ds(pl.multiple_of(to * dblock + g * half, half), half)],
            mblk.at[me, my_rows, my_cols],
            zm_s.at[r - 1],
            zm_r.at[r - 1],
            {"dp": to},
        )
        copy.start()
        zm.append(copy)

    acc = jnp.zeros((rows, cols), F32)
    for c in range(WCHUNKS):
        wcopies[c].wait()
        acc = acc + jnp.dot(
            merged[:, c * wrows : (c + 1) * wrows],
            w[c * wrows : (c + 1) * wrows, :],
            preferred_element_type=F32,
        )

    row_of = lax.broadcasted_iota(jnp.int32, (rows, 1), 0)
    valid = jnp.zeros((rows, 1), F32)
    for im in range(images):
        inside = (row_of >= im * per_image) & (row_of < (im + 1) * per_image)
        seen = inside & (4 * (row_of - im * per_image) < counts[im])
        valid = jnp.where(seen, 1.0, valid)
    masked[...] = acc.astype(BF16).astype(F32) * valid
    values = masked[...]

    wide = stat_out.shape[2]
    eye = lax.broadcasted_iota(jnp.int32, (rows, wide), 0) == lax.broadcasted_iota(
        jnp.int32, (rows, wide), 1
    )

    def send_stat(which, column):
        line = jnp.sum(jnp.where(eye, column, 0.0), axis=0, keepdims=True)
        line = jnp.broadcast_to(line, (8, wide))
        stat_out[which] = line
        stat_in[which, f] = line
        copies = []
        for q in range(1, shards):
            other = lax.rem(f + q, shards)
            copy = remote(
                stat_out.at[which],
                stat_in.at[which, f],
                st_s.at[which, q - 1],
                st_r.at[which, q - 1],
                at_plane(other // plane, lax.rem(other, plane)),
            )
            copy.start()
            copies.append(copy)
        return copies

    def take_stat(which, copies):
        for copy in copies:
            copy.wait()
        line = stat_in[which, 0]
        for other in range(1, shards):
            line = line + stat_in[which, other]
        return jnp.sum(jnp.where(eye, line[0:1], 0.0), axis=1, keepdims=True)

    squares = send_stat(0, jnp.sum(values * values, axis=1, keepdims=True))

    orow = own_row[...]
    hits = (orow == lax.broadcasted_iota(jnp.int32, (n, rows), 0)).astype(F32)
    i0 = lax.broadcasted_iota(jnp.int32, (rows, rows), 0)
    i1 = lax.broadcasted_iota(jnp.int32, (rows, rows), 1)
    upper = (i0 < i1).astype(F32).astype(BF16)
    before = jnp.dot(hits.astype(BF16), upper, preferred_element_type=F32)
    slot_row = jnp.sum(before * hits, axis=0, keepdims=True)
    tgt_row = orow * slots + slot_row.astype(jnp.int32)
    same = i0 == i1
    tgt_col = jnp.sum(jnp.where(same, tgt_row, 0), axis=1, keepdims=True)
    gain = gain_ref[...]

    def gather_place(p, target):
        ids = lax.broadcasted_iota(jnp.int32, (target.shape[0], slots), 1) + p * slots
        return (ids == target).astype(F32).astype(BF16)

    def scatter_place(target):
        ids = lax.broadcasted_iota(jnp.int32, (slots, rows), 0) + me * slots
        return (ids == target).astype(F32).astype(BF16)

    mblk[me] = merged[:, pl.ds(pl.multiple_of(me * dblock, dblock), dblock)]

    scale = lax.rsqrt(take_stat(0, squares) / D + 1e-05)
    emb[me] = jnp.dot(
        scatter_place(tgt_row),
        (values * scale * gain).astype(BF16),
        preferred_element_type=F32,
    ).astype(BF16)

    for t in range(1, n):
        for k in range(n):
            b = n - 1 - k

            @pl.when((me >= t) & (me < b))
            def _():
                cot_hop(me - t, b, 0).wait_recv()
                cot_hop(me - t, b, 0).start()

            @pl.when((me + t <= n - 1) & (me > k))
            def _():
                cot_hop(me + t, k, 1).wait_recv()
                cot_hop(me + t, k, 1).start()

    for t in range(1, n):

        @pl.when(me >= t)
        def _():
            cot_hop(me - t, me, 0).wait_recv()

        @pl.when(me + t <= n - 1)
        def _():
            cot_hop(me + t, me, 1).wait_recv()

    grads = jnp.zeros((rows, cols), F32)
    for p in range(n):
        grads = grads + jnp.dot(
            gather_place(p, tgt_col), cots[p, me], preferred_element_type=F32
        )
    grads = grads * gain
    values = masked[...]
    inners = send_stat(1, jnp.sum(grads * values, axis=1, keepdims=True))

    pm = []
    for r in range(1, n):
        zm[r - 1].wait()
        source = dp_of(n - r)
        for q in range(1, plane):
            piece = mblk.at[source, my_rows, my_cols]
            copy = remote(
                piece,
                piece,
                pm_s.at[r - 1, q - 1],
                pm_r.at[r - 1, q - 1],
                at_plane(g, lax.rem(st + q, plane)),
            )
            copy.start()
            pm.append(copy)

    inner = take_stat(1, inners) / D
    near = valid * scale
    far = valid * (scale * scale * scale * inner)
    back = (near * grads - values * far).astype(BF16)
    back_all[me] = back

    def as_line(column):
        return jnp.sum(jnp.where(eye, column, 0.0), axis=0, keepdims=True)

    info[me, 0:1] = as_line(tgt_col.astype(F32))
    info[me, 1:2] = as_line(scale)
    info[me, 2:3] = as_line(near)
    info[me, 3:4] = as_line(far)
    info[me, 4:8] = jnp.zeros((4, wide), F32)
    infos = []
    for r in range(1, n):
        copy = remote(
            info.at[me], info.at[me], in_s.at[r - 1], in_r.at[r - 1], {"dp": dp_of(r)}
        )
        copy.start()
        infos.append(copy)

    brows = rows // BCHUNKS

    def mix_hop(slot, b, c, side):
        piece = pl.ds(c * brows, brows)
        return remote(
            mix_out.at[slot, piece, :],
            mix.at[b, piece, :],
            mx_s.at[slot, c],
            mx_r.at[b, c],
            step_to(side),
        )

    packed = values.astype(BF16)
    mix_out[n] = jnp.where(tgt_col >= (me + 1) * slots, packed, back)
    mix_out[me] = jnp.where(tgt_col < me * slots, packed, back)
    for c in range(BCHUNKS):

        @pl.when(me < n - 1)
        def _():
            mix_hop(n, me, c, 0).start()

        @pl.when(me > 0)
        def _():
            mix_hop(me, me, c, 1).start()

    def take_block(b, side):
        def column(line):
            return jnp.sum(jnp.where(eye, info[b, line : line + 1], 0.0), axis=1, keepdims=True)

        target = column(0).astype(jnp.int32)
        r_scale, r_near, r_far = column(1), column(2), column(3)
        first, last = (me, n) if side == 0 else (0, me + 1)
        for c in range(BCHUNKS):
            lo, hi = c * brows, (c + 1) * brows
            aim = target[lo:hi]

            def add(p, total):
                return total + jnp.dot(
                    gather_place(p, aim), cots[p, b], preferred_element_type=F32
                )

            want = lax.fori_loop(first, last, add, jnp.zeros((brows, cols), F32)) * gain
            mix_hop(b, b, c, side).wait_recv()
            got = mix[b, lo:hi, :]
            whole = (r_near[lo:hi] * want - got.astype(F32) * r_far[lo:hi]).astype(BF16)
            if side == 0:
                whole = jnp.where(aim >= me * slots, whole, got)
                onward = jnp.where(aim >= (me + 1) * slots, got, whole)
                more = me < n - 1
            else:
                whole = jnp.where(aim < (me + 1) * slots, whole, got)
                onward = jnp.where(aim < me * slots, got, whole)
                more = me > 0
            back_all[b, lo:hi, :] = whole
            mix_out[b, lo:hi, :] = onward

            @pl.when(more)
            def _():
                mix_hop(b, b, c, side).start()

        line = info[b, 0:1, 0:rows].astype(jnp.int32)
        emb[b] = jnp.dot(
            scatter_place(line),
            (mix[b].astype(F32) * r_scale * gain).astype(BF16),
            preferred_element_type=F32,
        ).astype(BF16)

    def take_blocks(t):
        @pl.when(me >= t)
        def _():
            take_block(me - t, 0)

        @pl.when(me + t <= n - 1)
        def _():
            take_block(me + t, 1)

    gm_copies = []
    for r in range(1, n):
        for q in range(1, plane):
            pm[(r - 1) * (plane - 1) + q - 1].wait()
        piece = mblk.at[dp_of(n - r), :, my_cols]
        copy = remote(piece, piece, gm_s.at[r - 1], gm_r.at[r - 1], {"group": 1 - g})
        copy.start()
        gm_copies.append(copy)

    def partial(gg, ss):
        start = pl.multiple_of((gg * plane + ss) * gcols, gcols)
        return lax.dot_general(
            back_all[me],
            w[pl.ds(start, gcols), :],
            (((1,), (1,)), ((), ())),
            preferred_element_type=F32,
        )

    po = []
    for q in range(plane):
        slot = (q + 1) % plane
        pair_out[slot] = partial(1 - g, lax.rem(st + slot, plane)).astype(BF16)
        copy = remote(
            pair_out.at[slot], pair_in.at[slot], po_s.at[slot], po_r.at[slot], {"group": 1 - g}
        )
        copy.start()
        po.append(copy)
    for copy in infos:
        copy.wait()
    take_blocks(1)
    ps = []
    for q in range(plane):
        slot = (q + 1) % plane
        mine = partial(g, lax.rem(st + slot, plane))
        po[q].wait()
        mine = mine + pair_in[slot].astype(F32)
        if slot == 0:
            gm[...] = mine
        else:
            plane_out[slot - 1] = mine.astype(BF16)
            copy = remote(
                plane_out.at[slot - 1],
                plane_in.at[slot - 1],
                pl_s.at[slot - 1],
                pl_r.at[slot - 1],
                at_plane(g, lax.rem(st + slot, plane)),
            )
            copy.start()
            ps.append(copy)

    for t in range(2, n):
        take_blocks(t)

    for copy in ps:
        copy.wait()
    total = gm[...]
    for q in range(plane - 1):
        total = total + plane_in[q].astype(F32)
    gm[...] = total
    for copy in gm_copies:
        copy.wait()
    for t in range(n):
        for k in range(n):
            b = n - 1 - k

            @pl.when((me >= t) & (me < b))
            def _():
                cot_hop(me - t, b, 0).wait_send()

            @pl.when((me + t <= n - 1) & (me > k))
            def _():
                cot_hop(me + t, k, 1).wait_send()

        for c in range(BCHUNKS):

            @pl.when((me >= t) & (me < n - 1))
            def _():
                mix_hop(n if t == 0 else me - t, me - t, c, 0).wait_send()

            @pl.when((me + t <= n - 1) & (me > 0))
            def _():
                mix_hop(me + t, me + t, c, 1).wait_send()


def weight_kernel(m_ref, b_ref, o_ref):
    o_ref[...] = lax.dot_general(
        m_ref[...], b_ref[...], (((0,), (0,)), ((), ())), preferred_element_type=F32
    )


def fast(sizes, merged, counts, owners, w_merge, norm_gain, cotangent):
    n, groups, sections, tensors = sizes
    plane = sections * tensors
    shards = groups * plane
    rows, deep = merged.shape
    cols = w_merge.shape[1]
    slots = cotangent.shape[2]
    dblock = deep // n
    gcols = deep // shards
    wide = -(-rows // 128) * 128
    vmem = pl.BlockSpec(memory_space=pltpu.VMEM)
    dma = pltpu.SemaphoreType.DMA
    emb, gm, mblk, back_all = pl.pallas_call(
        functools.partial(main_kernel, sizes),
        name="exchange",
        out_shape=(
            jax.ShapeDtypeStruct((n, slots, cols), BF16),
            jax.ShapeDtypeStruct((rows, gcols), F32),
            jax.ShapeDtypeStruct((n, rows, dblock), BF16),
            jax.ShapeDtypeStruct((n, rows, cols), BF16),
        ),
        in_specs=[
            vmem,
            pl.BlockSpec(memory_space=pltpu.SMEM),
            vmem,
            pl.BlockSpec(memory_space=pl.ANY),
            vmem,
            pl.BlockSpec(memory_space=pl.ANY),
        ],
        out_specs=(vmem, vmem, vmem, vmem),
        scratch_shapes=[
            pltpu.VMEM((deep, cols), BF16),
            pltpu.VMEM((n, n, slots, cols), BF16),
            pltpu.VMEM((n, rows, cols), BF16),
            pltpu.VMEM((n + 1, rows, cols), BF16),
            pltpu.VMEM((n, 8, wide), F32),
            pltpu.VMEM((rows, cols), F32),
            pltpu.VMEM((2, 8, wide), F32),
            pltpu.VMEM((2, shards, 8, wide), F32),
            pltpu.VMEM((plane, rows, gcols), BF16),
            pltpu.VMEM((plane, rows, gcols), BF16),
            pltpu.VMEM((plane - 1, rows, gcols), BF16),
            pltpu.VMEM((plane - 1, rows, gcols), BF16),
            dma((WCHUNKS,)),
            dma,
            dma((n - 1,)),
            dma((n - 1,)),
            dma((n, n)),
            dma((n, n)),
            dma((n - 1,)),
            dma((n - 1,)),
            dma((2, shards - 1)),
            dma((2, shards - 1)),
            dma((n - 1, plane - 1)),
            dma((n - 1, plane - 1)),
            dma((n - 1,)),
            dma((n - 1,)),
            dma((n + 1, BCHUNKS)),
            dma((n, BCHUNKS)),
            dma((plane,)),
            dma((plane,)),
            dma((plane - 1,)),
            dma((plane - 1,)),
        ],
        compiler_params=pltpu.CompilerParams(collective_id=0, has_side_effects=True),
    )(
        owners.reshape(1, rows),
        counts,
        merged,
        w_merge,
        norm_gain.reshape(1, cols),
        cotangent[0],
    )
    tile = 256
    grad_weight = pl.pallas_call(
        weight_kernel,
        name="weight",
        grid=(dblock // tile,),
        out_shape=jax.ShapeDtypeStruct((dblock, cols), F32),
        in_specs=[
            pl.BlockSpec((n * rows, tile), lambda i: (0, i)),
            pl.BlockSpec((n * rows, cols), lambda i: (0, 0)),
        ],
        out_specs=pl.BlockSpec((tile, cols), lambda i: (i, 0)),
    )(mblk.reshape(n * rows, dblock), back_all.reshape(n * rows, cols))
    return emb[None], gm, grad_weight


def solution(mesh):
    sizes = tuple(mesh.shape[name] for name in ("dp", "group", "section", "tensor"))

    def choose(merged, counts, owners, w_merge, norm_gain, cotangent):
        n, groups, sections, tensors = sizes
        plane = sections * tensors
        rows, deep = merged.shape
        cols = w_merge.shape[1]
        slots = cotangent.shape[2]
        fits = (
            groups == 2
            and n > 1
            and plane > 1
            and rows % (plane * 16) == 0
            and rows % (BCHUNKS * 16) == 0
            and deep % (n * groups * 128) == 0
            and deep % (n * 256) == 0
            and deep % (groups * plane * 128) == 0
            and deep % (WCHUNKS * 128) == 0
            and cols % 128 == 0
            and slots % 16 == 0
        )
        if fits:
            return fast(sizes, merged, counts, owners, w_merge, norm_gain, cotangent)
        return on_device(merged, counts, owners, w_merge, norm_gain, cotangent)

    placed = (
        P("dp", None),
        P("dp"),
        P("dp", None),
        P(None, ("group", "section", "tensor")),
        P(("group", "section", "tensor")),
        P("dp", None, None, ("group", "section", "tensor")),
    )
    return jax.shard_map(
        choose,
        mesh=mesh,
        in_specs=placed,
        out_specs=(
            P("dp", None, None, ("group", "section", "tensor")),
            P("dp", ("group", "section", "tensor")),
            P("dp", ("group", "section", "tensor")),
        ),
        check_vma=False,
    )
```

```python
import functools

import jax
import jax.numpy as jnp
from jax import lax
from jax.experimental import pallas as pl
from jax.experimental.pallas import tpu as pltpu
from jax.sharding import PartitionSpec as P

D = 8192
MESH = pl.DeviceIdType.MESH
F32 = jnp.float32
BF16 = jnp.bfloat16
WCHUNKS = 5
BCHUNKS = 2
TILE = 256


def on_device(merged, counts, owners, w_merge, norm_gain, cotangent):
    rows = merged.shape[0]
    columns = w_merge.shape[1]
    replicas = lax.axis_size("dp")
    slots = cotangent.shape[2]
    images = counts.shape[0]
    per_image = rows // images
    projected = jnp.dot(merged, w_merge, preferred_element_type=jnp.float32).astype(jnp.bfloat16)
    row_index = jnp.arange(rows, dtype=jnp.int32)
    image_of = row_index // per_image
    picked = image_of[:, None] == jnp.arange(images, dtype=jnp.int32)[None, :]
    count_of = jnp.sum(jnp.where(picked, counts[None, :], 0), axis=1)
    valid = (4 * (row_index % per_image) < count_of).astype(jnp.float32)
    masked = (projected.astype(jnp.float32) * valid[:, None]).astype(jnp.bfloat16)
    owner = owners[:, 0]
    hits = (owner[:, None] == jnp.arange(replicas, dtype=jnp.int32)[None, :]).astype(jnp.int32)
    before = jnp.cumsum(hits, axis=0) - hits
    slot_index = jnp.sum(before * hits, axis=1)
    target = owner * slots + slot_index
    placer = (jnp.arange(replicas * slots, dtype=jnp.int32)[:, None] == target[None, :]).astype(
        jnp.bfloat16
    )
    outgoing = jnp.dot(placer, masked, preferred_element_type=jnp.float32).astype(jnp.bfloat16)
    outgoing = outgoing.reshape(replicas, slots, columns)
    received = lax.all_to_all(outgoing, "dp", split_axis=0, concat_axis=0, tiled=True)
    values = received.astype(jnp.float32)
    square_sums = lax.psum(jnp.sum(values * values, axis=2), ("group", "section", "tensor"))
    scale = lax.rsqrt(square_sums / D + 1e-05)
    normed = (values * scale[:, :, None] * norm_gain[None, None, :]).astype(jnp.bfloat16)
    embedded = normed[None]
    grad_in = cotangent[0].astype(jnp.float32) * norm_gain[None, None, :]
    inner_sums = lax.psum(jnp.sum(grad_in * values, axis=2), ("group", "section", "tensor"))
    inner = inner_sums / D
    slot_grad = (scale[:, :, None] * grad_in - values * (scale**3 * inner)[:, :, None]).astype(
        jnp.bfloat16
    )
    returned = lax.all_to_all(slot_grad, "dp", split_axis=0, concat_axis=0, tiled=True)
    returned = returned.reshape(replicas * slots, columns)
    gathered = lax.dot_general(
        placer, returned, (((0,), (0,)), ((), ())), preferred_element_type=jnp.float32
    )
    back = (gathered * valid[:, None]).astype(jnp.bfloat16)
    input_terms = lax.dot_general(
        back, w_merge, (((1,), (1,)), ((), ())), preferred_element_type=jnp.float32
    )
    grad_merged = lax.psum_scatter(
        input_terms, ("group", "section", "tensor"), scatter_dimension=1, tiled=True
    )
    column_block = lax.all_to_all(merged, "dp", split_axis=1, concat_axis=0, tiled=True)
    grad_weight = lax.dot_general(
        column_block,
        lax.all_gather(back, "dp", axis=0, tiled=True),
        (((0,), (0,)), ((), ())),
        preferred_element_type=jnp.float32,
    )
    return (embedded, grad_merged, grad_weight)


def remote(src, dst, send_sem, recv_sem, device):
    return pltpu.make_async_remote_copy(
        src_ref=src,
        dst_ref=dst,
        send_sem=send_sem,
        recv_sem=recv_sem,
        device_id=device,
        device_id_type=MESH,
    )


def main_kernel(
    sizes,
    own_row,
    counts,
    merged,
    w_hbm,
    gain_ref,
    cot_hbm,
    emb,
    gm,
    mblk,
    back_all,
    w,
    cots,
    mix,
    mix_out,
    info,
    masked,
    stat_out,
    stat_in,
    pair_out,
    pair_in,
    plane_out,
    plane_in,
    w_sem,
    cot_sem,
    zm_s,
    zm_r,
    ck_s,
    ck_r,
    in_s,
    in_r,
    st_s,
    st_r,
    pm_s,
    pm_r,
    gm_s,
    gm_r,
    mx_s,
    mx_r,
    po_s,
    po_r,
    pl_s,
    pl_r,
):
    n, groups, sections, tensors = sizes
    plane = sections * tensors
    shards = groups * plane
    rows, deep = merged.shape
    cols = w.shape[1]
    slots = cots.shape[2]
    dblock = deep // n
    half = dblock // groups
    part = rows // plane
    gcols = deep // shards
    images = counts.shape[0]
    per_image = rows // images
    me = lax.axis_index("dp")
    g = lax.axis_index("group")
    st = lax.axis_index("section") * tensors + lax.axis_index("tensor")
    f = g * plane + st

    def dp_of(r):
        return lax.rem(me + r, n)

    def at_plane(gg, ss):
        return {"group": gg, "section": ss // tensors, "tensor": lax.rem(ss, tensors)}

    barrier = pltpu.get_barrier_semaphore()
    for r in range(1, n):
        pl.semaphore_signal(barrier, inc=1, device_id={"dp": dp_of(r)}, device_id_type=MESH)
    for q in range(1, shards):
        other = lax.rem(f + q, shards)
        pl.semaphore_signal(
            barrier,
            inc=1,
            device_id=at_plane(other // plane, lax.rem(other, plane)),
            device_id_type=MESH,
        )
    cot_load = pltpu.make_async_copy(cot_hbm, cots.at[me], cot_sem)
    cot_load.start()
    wrows = deep // WCHUNKS
    wcopies = []
    for c in range(WCHUNKS):
        copy = pltpu.make_async_copy(
            w_hbm.at[pl.ds(c * wrows, wrows), :], w.at[pl.ds(c * wrows, wrows), :], w_sem.at[c]
        )
        copy.start()
        wcopies.append(copy)
    pl.semaphore_wait(barrier, n - 1 + shards - 1)

    my_rows = pl.ds(pl.multiple_of(st * part, part), part)
    my_cols = pl.ds(pl.multiple_of(g * half, half), half)
    def step_to(side):
        return {"dp": jnp.clip(me + (1 if side == 0 else -1), 0, n - 1)}

    def cot_hop(p, b, side, own=False):
        piece = cots.at[p, b]
        return remote(cot_hbm.at[b] if own else piece, piece, ck_s.at[p, b], ck_r.at[p, b], step_to(side))

    for k in range(n - 1):
        b = n - 1 - k

        @pl.when(me < b)
        def _():
            cot_hop(me, b, 0, True).start()

        @pl.when(me > k)
        def _():
            cot_hop(me, k, 1, True).start()

    acc = jnp.zeros((rows, cols), F32)
    for c in range(WCHUNKS):
        wcopies[c].wait()
        acc = acc + jnp.dot(
            merged[:, c * wrows : (c + 1) * wrows],
            w[c * wrows : (c + 1) * wrows, :],
            preferred_element_type=F32,
        )

    row_of = lax.broadcasted_iota(jnp.int32, (rows, 1), 0)
    valid = jnp.zeros((rows, 1), F32)
    for im in range(images):
        inside = (row_of >= im * per_image) & (row_of < (im + 1) * per_image)
        seen = inside & (4 * (row_of - im * per_image) < counts[im])
        valid = jnp.where(seen, 1.0, valid)
    masked[...] = acc.astype(BF16).astype(F32) * valid
    values = masked[...]

    wide = stat_out.shape[2]
    eye = lax.broadcasted_iota(jnp.int32, (rows, wide), 0) == lax.broadcasted_iota(
        jnp.int32, (rows, wide), 1
    )

    def send_stat(which, column):
        line = jnp.sum(jnp.where(eye, column, 0.0), axis=0, keepdims=True)
        line = jnp.broadcast_to(line, (8, wide))
        stat_out[which] = line
        stat_in[which, f] = line
        copies = []
        for q in range(1, shards):
            other = lax.rem(f + q, shards)
            copy = remote(
                stat_out.at[which],
                stat_in.at[which, f],
                st_s.at[which, q - 1],
                st_r.at[which, q - 1],
                at_plane(other // plane, lax.rem(other, plane)),
            )
            copy.start()
            copies.append(copy)
        return copies

    def take_stat(which, copies):
        for copy in copies:
            copy.wait()
        line = stat_in[which, 0]
        for other in range(1, shards):
            line = line + stat_in[which, other]
        return jnp.sum(jnp.where(eye, line[0:1], 0.0), axis=1, keepdims=True)

    squares = send_stat(0, jnp.sum(values * values, axis=1, keepdims=True))

    orow = own_row[...]
    hits = (orow == lax.broadcasted_iota(jnp.int32, (n, rows), 0)).astype(F32)
    i0 = lax.broadcasted_iota(jnp.int32, (rows, rows), 0)
    i1 = lax.broadcasted_iota(jnp.int32, (rows, rows), 1)
    upper = (i0 < i1).astype(F32).astype(BF16)
    before = jnp.dot(hits.astype(BF16), upper, preferred_element_type=F32)
    slot_row = jnp.sum(before * hits, axis=0, keepdims=True)
    tgt_row = orow * slots + slot_row.astype(jnp.int32)
    same = i0 == i1
    tgt_col = jnp.sum(jnp.where(same, tgt_row, 0), axis=1, keepdims=True)
    gain = gain_ref[...]

    def gather_place(p, target):
        ids = lax.broadcasted_iota(jnp.int32, (target.shape[0], slots), 1) + p * slots
        return (ids == target).astype(F32).astype(BF16)

    def scatter_place(target):
        ids = lax.broadcasted_iota(jnp.int32, (slots, rows), 0) + me * slots
        return (ids == target).astype(F32).astype(BF16)

    mblk[me] = merged[:, pl.ds(pl.multiple_of(me * dblock, dblock), dblock)]

    scale = lax.rsqrt(take_stat(0, squares) / D + 1e-05)
    emb[me] = jnp.dot(
        scatter_place(tgt_row),
        (values * scale * gain).astype(BF16),
        preferred_element_type=F32,
    ).astype(BF16)

    for t in range(1, n):
        for k in range(n):
            b = n - 1 - k

            @pl.when((me >= t) & (me < b))
            def _():
                cot_hop(me - t, b, 0).wait_recv()
                cot_hop(me - t, b, 0).start()

            @pl.when((me + t <= n - 1) & (me > k))
            def _():
                cot_hop(me + t, k, 1).wait_recv()
                cot_hop(me + t, k, 1).start()

    zm = []
    for r in range(1, n):
        to = dp_of(r)
        copy = remote(
            merged.at[my_rows, pl.ds(pl.multiple_of(to * dblock + g * half, half), half)],
            mblk.at[me, my_rows, my_cols],
            zm_s.at[r - 1],
            zm_r.at[r - 1],
            {"dp": to},
        )
        copy.start()
        zm.append(copy)

    for t in range(1, n):

        @pl.when(me >= t)
        def _():
            cot_hop(me - t, me, 0).wait_recv()

        @pl.when(me + t <= n - 1)
        def _():
            cot_hop(me + t, me, 1).wait_recv()

    cot_load.wait()
    grads = jnp.zeros((rows, cols), F32)
    for p in range(n):
        grads = grads + jnp.dot(
            gather_place(p, tgt_col), cots[p, me], preferred_element_type=F32
        )
    grads = grads * gain
    values = masked[...]
    inners = send_stat(1, jnp.sum(grads * values, axis=1, keepdims=True))

    pm = []
    for r in range(1, n):
        zm[r - 1].wait()
        source = dp_of(n - r)
        for q in range(1, plane):
            piece = mblk.at[source, my_rows, my_cols]
            copy = remote(
                piece,
                piece,
                pm_s.at[r - 1, q - 1],
                pm_r.at[r - 1, q - 1],
                at_plane(g, lax.rem(st + q, plane)),
            )
            copy.start()
            pm.append(copy)

    inner = take_stat(1, inners) / D
    near = valid * scale
    far = valid * (scale * scale * scale * inner)
    back = (near * grads - values * far).astype(BF16)
    back_all[me] = back

    def as_line(column):
        return jnp.sum(jnp.where(eye, column, 0.0), axis=0, keepdims=True)

    info[me, 0:1] = as_line(tgt_col.astype(F32))
    info[me, 1:2] = as_line(scale)
    info[me, 2:3] = as_line(near)
    info[me, 3:4] = as_line(far)
    info[me, 4:8] = jnp.zeros((4, wide), F32)
    infos = []
    for r in range(1, n):
        copy = remote(
            info.at[me], info.at[me], in_s.at[r - 1], in_r.at[r - 1], {"dp": dp_of(r)}
        )
        copy.start()
        infos.append(copy)

    brows = rows // BCHUNKS

    def mix_hop(slot, b, c, side):
        piece = pl.ds(c * brows, brows)
        return remote(
            mix_out.at[slot, piece, :],
            mix.at[b, piece, :],
            mx_s.at[slot, c],
            mx_r.at[b, c],
            step_to(side),
        )

    packed = values.astype(BF16)
    mix_out[n] = jnp.where(tgt_col >= (me + 1) * slots, packed, back)
    mix_out[me] = jnp.where(tgt_col < me * slots, packed, back)
    for c in range(BCHUNKS):

        @pl.when(me < n - 1)
        def _():
            mix_hop(n, me, c, 0).start()

        @pl.when(me > 0)
        def _():
            mix_hop(me, me, c, 1).start()

    def take_chunk(b, side, c):
        lo, hi = c * brows, (c + 1) * brows

        def column(line):
            picked = jnp.where(eye[lo:hi], info[b, line : line + 1], 0.0)
            return jnp.sum(picked, axis=1, keepdims=True)

        aim = column(0).astype(jnp.int32)
        r_near, r_far = column(2), column(3)
        first, last = (me, n) if side == 0 else (0, me + 1)

        def add(p, total):
            return total + jnp.dot(
                gather_place(p, aim), cots[p, b], preferred_element_type=F32
            )

        want = lax.fori_loop(first, last, add, jnp.zeros((brows, cols), F32)) * gain * r_near
        mix_hop(b, b, c, side).wait_recv()
        got = mix[b, lo:hi, :]
        whole = (want - got.astype(F32) * r_far).astype(BF16)
        if side == 0:
            whole = jnp.where(aim >= me * slots, whole, got)
            onward = jnp.where(aim >= (me + 1) * slots, got, whole)
            more = me < n - 1
        else:
            whole = jnp.where(aim < (me + 1) * slots, whole, got)
            onward = jnp.where(aim < me * slots, got, whole)
            more = me > 0
        mix_out[b, lo:hi, :] = onward

        @pl.when(more)
        def _():
            mix_hop(b, b, c, side).start()

        back_all[b, lo:hi, :] = whole

    def embed(b):
        r_scale = jnp.sum(jnp.where(eye, info[b, 1:2], 0.0), axis=1, keepdims=True)
        line = info[b, 0:1, 0:rows].astype(jnp.int32)
        emb[b] = jnp.dot(
            scatter_place(line),
            (mix[b].astype(F32) * r_scale * gain).astype(BF16),
            preferred_element_type=F32,
        ).astype(BF16)

    def take_blocks(t):
        for c in range(BCHUNKS):

            @pl.when(me >= t)
            def _():
                take_chunk(me - t, 0, c)

            @pl.when(me + t <= n - 1)
            def _():
                take_chunk(me + t, 1, c)

        @pl.when(me >= t)
        def _():
            embed(me - t)

        @pl.when(me + t <= n - 1)
        def _():
            embed(me + t)

    gm_copies = []
    for r in range(1, n):
        for q in range(1, plane):
            pm[(r - 1) * (plane - 1) + q - 1].wait()
        piece = mblk.at[dp_of(n - r), :, my_cols]
        copy = remote(piece, piece, gm_s.at[r - 1], gm_r.at[r - 1], {"group": 1 - g})
        copy.start()
        gm_copies.append(copy)

    def partial(gg, ss):
        start = pl.multiple_of((gg * plane + ss) * gcols, gcols)
        return lax.dot_general(
            back_all[me],
            w[pl.ds(start, gcols), :],
            (((1,), (1,)), ((), ())),
            preferred_element_type=F32,
        )

    po = []
    for q in range(plane):
        slot = (q + 1) % plane
        pair_out[slot] = partial(1 - g, lax.rem(st + slot, plane)).astype(BF16)
        copy = remote(
            pair_out.at[slot], pair_in.at[slot], po_s.at[slot], po_r.at[slot], {"group": 1 - g}
        )
        copy.start()
        po.append(copy)
    for copy in infos:
        copy.wait()
    take_blocks(1)
    ps = []
    for q in range(plane):
        slot = (q + 1) % plane
        mine = partial(g, lax.rem(st + slot, plane))
        po[q].wait()
        mine = mine + pair_in[slot].astype(F32)
        if slot == 0:
            gm[...] = mine
        else:
            plane_out[slot - 1] = mine.astype(BF16)
            copy = remote(
                plane_out.at[slot - 1],
                plane_in.at[slot - 1],
                pl_s.at[slot - 1],
                pl_r.at[slot - 1],
                at_plane(g, lax.rem(st + slot, plane)),
            )
            copy.start()
            ps.append(copy)

    for t in range(2, n):
        take_blocks(t)

    for copy in ps:
        copy.wait()
    total = gm[...]
    for q in range(plane - 1):
        total = total + plane_in[q].astype(F32)
    gm[...] = total
    for copy in gm_copies:
        copy.wait()
    for t in range(n):
        for k in range(n):
            b = n - 1 - k

            @pl.when((me >= t) & (me < b))
            def _():
                cot_hop(me - t, b, 0).wait_send()

            @pl.when((me + t <= n - 1) & (me > k))
            def _():
                cot_hop(me + t, k, 1).wait_send()

        for c in range(BCHUNKS):

            @pl.when((me >= t) & (me < n - 1))
            def _():
                mix_hop(n if t == 0 else me - t, me - t, c, 0).wait_send()

            @pl.when((me + t <= n - 1) & (me > 0))
            def _():
                mix_hop(me + t, me + t, c, 1).wait_send()


def weight_kernel(m_ref, b_ref, e_ref, g_ref, o_ref, eo_ref, go_ref):
    o_ref[...] = lax.dot_general(
        m_ref[...], b_ref[...], (((0,), (0,)), ((), ())), preferred_element_type=F32
    )
    eo_ref[...] = e_ref[...]
    go_ref[...] = g_ref[...]


def fast(sizes, merged, counts, owners, w_merge, norm_gain, cotangent):
    n, groups, sections, tensors = sizes
    plane = sections * tensors
    shards = groups * plane
    rows, deep = merged.shape
    cols = w_merge.shape[1]
    slots = cotangent.shape[2]
    dblock = deep // n
    gcols = deep // shards
    wide = -(-rows // 128) * 128
    vmem = pl.BlockSpec(memory_space=pltpu.VMEM)
    dma = pltpu.SemaphoreType.DMA
    emb, gm, mblk, back_all = pl.pallas_call(
        functools.partial(main_kernel, sizes),
        name="exchange",
        out_shape=(
            jax.ShapeDtypeStruct((n, slots, cols), BF16),
            jax.ShapeDtypeStruct((rows, gcols), F32),
            jax.ShapeDtypeStruct((n, rows, dblock), BF16),
            jax.ShapeDtypeStruct((n, rows, cols), BF16),
        ),
        in_specs=[
            vmem,
            pl.BlockSpec(memory_space=pltpu.SMEM),
            vmem,
            pl.BlockSpec(memory_space=pl.ANY),
            vmem,
            pl.BlockSpec(memory_space=pl.ANY),
        ],
        out_specs=(vmem, vmem, vmem, vmem),
        scratch_shapes=[
            pltpu.VMEM((deep, cols), BF16),
            pltpu.VMEM((n, n, slots, cols), BF16),
            pltpu.VMEM((n, rows, cols), BF16),
            pltpu.VMEM((n + 1, rows, cols), BF16),
            pltpu.VMEM((n, 8, wide), F32),
            pltpu.VMEM((rows, cols), F32),
            pltpu.VMEM((2, 8, wide), F32),
            pltpu.VMEM((2, shards, 8, wide), F32),
            pltpu.VMEM((plane, rows, gcols), BF16),
            pltpu.VMEM((plane, rows, gcols), BF16),
            pltpu.VMEM((plane - 1, rows, gcols), BF16),
            pltpu.VMEM((plane - 1, rows, gcols), BF16),
            dma((WCHUNKS,)),
            dma,
            dma((n - 1,)),
            dma((n - 1,)),
            dma((n, n)),
            dma((n, n)),
            dma((n - 1,)),
            dma((n - 1,)),
            dma((2, shards - 1)),
            dma((2, shards - 1)),
            dma((n - 1, plane - 1)),
            dma((n - 1, plane - 1)),
            dma((n - 1,)),
            dma((n - 1,)),
            dma((n + 1, BCHUNKS)),
            dma((n, BCHUNKS)),
            dma((plane,)),
            dma((plane,)),
            dma((plane - 1,)),
            dma((plane - 1,)),
        ],
        compiler_params=pltpu.CompilerParams(collective_id=0, has_side_effects=True),
    )(
        owners.reshape(1, rows),
        counts,
        merged,
        w_merge,
        norm_gain.reshape(1, cols),
        cotangent[0],
    )
    tile = TILE
    steps = dblock // tile
    pieces = 1
    while pieces * 2 <= steps and (rows // (pieces * 2)) % 8 == 0:
        pieces *= 2
    egot, ggot = n * slots // pieces, rows // pieces

    def piece_map(i):
        return (jnp.minimum(i, pieces - 1), 0)

    grad_weight, emb, gm = pl.pallas_call(
        weight_kernel,
        name="weight",
        grid=(steps,),
        out_shape=(
            jax.ShapeDtypeStruct((dblock, cols), F32),
            jax.ShapeDtypeStruct((n * slots, cols), BF16),
            jax.ShapeDtypeStruct((rows, gcols), F32),
        ),
        in_specs=[
            pl.BlockSpec((n * rows, tile), lambda i: (0, i)),
            pl.BlockSpec((n * rows, cols), lambda i: (0, 0)),
            pl.BlockSpec((egot, cols), piece_map),
            pl.BlockSpec((ggot, gcols), piece_map),
        ],
        out_specs=(
            pl.BlockSpec((tile, cols), lambda i: (i, 0)),
            pl.BlockSpec((egot, cols), piece_map),
            pl.BlockSpec((ggot, gcols), piece_map),
        ),
    )(
        mblk.reshape(n * rows, dblock),
        back_all.reshape(n * rows, cols),
        emb.reshape(n * slots, cols),
        gm,
    )
    return emb.reshape(1, n, slots, cols), gm, grad_weight


def solution(mesh):
    sizes = tuple(mesh.shape[name] for name in ("dp", "group", "section", "tensor"))

    def choose(merged, counts, owners, w_merge, norm_gain, cotangent):
        n, groups, sections, tensors = sizes
        plane = sections * tensors
        rows, deep = merged.shape
        cols = w_merge.shape[1]
        slots = cotangent.shape[2]
        fits = (
            groups == 2
            and n > 1
            and plane > 1
            and rows % (plane * 16) == 0
            and rows % (BCHUNKS * 16) == 0
            and deep % (n * groups * 128) == 0
            and deep % (n * TILE) == 0
            and deep % (groups * plane * 128) == 0
            and deep % (WCHUNKS * 128) == 0
            and cols % 128 == 0
            and slots % 16 == 0
            and (n * slots) % rows == 0
        )
        if fits:
            return fast(sizes, merged, counts, owners, w_merge, norm_gain, cotangent)
        return on_device(merged, counts, owners, w_merge, norm_gain, cotangent)

    placed = (
        P("dp", None),
        P("dp"),
        P("dp", None),
        P(None, ("group", "section", "tensor")),
        P(("group", "section", "tensor")),
        P("dp", None, None, ("group", "section", "tensor")),
    )
    return jax.shard_map(
        choose,
        mesh=mesh,
        in_specs=placed,
        out_specs=(
            P("dp", None, None, ("group", "section", "tensor")),
            P("dp", ("group", "section", "tensor")),
            P("dp", ("group", "section", "tensor")),
        ),
        check_vma=False,
    )
```
